32 devices in a mesh: groups: 2 (over y), enc: 4 (over z), dec: 2 (over x), mp: 2 (over core).
Axes of the slice: x: 2, y: 2, z: 4, core: 2. Of those that a mesh axis runs over, the one named last changes fastest.
Arguments:
- tokens: bfloat16 [4, 16, 16, 16, 1280], P(('groups', 'dec'), 'enc'), parts along dimension 0, may hold values from -6 to 6
- gain_pre: float32 [1280], replicated, may hold values from 0.5 to 2
- w_up: bfloat16 [1280, 2560], P('enc', 'mp'), may hold values from -0.15625 to 0.15625
- w_down: bfloat16 [2560, 1280], P('mp', 'enc'), may hold values from -0.125 to 0.125
- gain_post: float32 [1280], replicated, may hold values from 0.5 to 2
- w_neck: bfloat16 [1280, 256], replicated, may hold values from -0.15625 to 0.15625
- conv_weight: bfloat16 [3, 3, 256, 256], P(None, None, None, 'mp'), may hold values from -0.125 to 0.125
- conv_bias: float32 [256], P('mp'), may hold values from -3 to 3
- cls_weight: bfloat16 [256, 13], P('mp'), may hold values from -0.375 to 0.375
- cls_bias: float32 [13], replicated, may hold values from -4 to 4
- tile_table: int32 [4, 16, 2], P(('groups', 'dec')), parts along dimension 0, may hold values from -1 to 16, as said below
- labels: int32 [8, 4, 96], P(None, 'enc', ('groups', 'dec')), parts along dimension 2, may hold values from 0 to 12
Outputs:
- logits: float32 [8, 4, 96, 13], P(None, 'enc', ('groups', 'dec')), parts along dimension 2
- nll: float32 [8, 4, 96], P(None, 'enc', ('groups', 'dec')), parts along dimension 2
The draws below stay inside these ranges and needn't reach their ends.
There are 2 independent parts, one for each index of `groups`. The reference program is written for one: setup_inputs(seed, part) draws one part's arguments, and reference() takes and returns one part's arrays. A program takes and returns all parts, laid end to end along the dimension named above; an argument that names none is the same for every part. Nothing has to cross between parts.
Inputs may be any that keep to these rules, and one draw needn't show every extreme that they name: `tile_table`: in every band each tile corner with strip row a multiple of 8 from 0 to 16 and band column 0 or 8 stands in exactly one slot; all other slots are empty; in every band one encoder rank holds 4 tiles.
All inputs are finite; a program needn't handle non-finite values.
Results may differ from the reference program's by a relative error of at most 0.0075.
Values may be sent and summed in bfloat16 or wider, within the bound.
No kernel may reach another device: no remote copies, remote signals or barrier semaphores. Data moves between devices by JAX's collectives and lax.ppermute only.
A program may use at most 64 MiB of HBM per device.

```python
import math
import jax
import jax.numpy as jnp
from jax import lax

D = 1280
FF = 2560
C = 256
NCLS = 13
TS = 16
BAND = 24
TSLOT = 4
RS = 8
W_ALL = 48
N_ENC = 4
N_DEC = 2
N_MP = 2


def draw_tile_table(key, part):
    slots_all = N_ENC * TSLOT
    rows_strip = RS * N_ENC
    stride = TS // 2
    tile_total = 2 * ((rows_strip - TS) // stride + 1)
    band_keys = jax.random.split(jax.random.fold_in(key, 7), N_DEC)

    def one_band(band_key):
        key_order, key_heavy, key_spread = jax.random.split(band_key, 3)
        tile_order = jax.random.permutation(key_order, tile_total).astype(jnp.int32)
        heavy_rank = jax.random.randint(key_heavy, (), 0, N_ENC).astype(jnp.int32)
        spread = jax.random.permutation(key_spread, slots_all - TSLOT).astype(jnp.int32)
        others = spread[:tile_total - TSLOT]
        others = jnp.where(others < heavy_rank * TSLOT, others, others + TSLOT)
        slot_of = jnp.concatenate([heavy_rank * TSLOT + jnp.arange(TSLOT, dtype=jnp.int32), others])
        tile_rows = (stride * (tile_order // 2)).astype(jnp.int32)
        tile_cols = (stride * (tile_order % 2)).astype(jnp.int32)
        slot_table = jnp.full((slots_all, 2), -1, jnp.int32)
        slot_table = slot_table.at[slot_of, 0].set(tile_rows)
        slot_table = slot_table.at[slot_of, 1].set(tile_cols)
        return slot_table
    return jax.vmap(one_band)(band_keys)


def with_ends(entries, rng, low, largest):
    dims = entries.shape
    place = [jax.random.randint(jax.random.fold_in(rng, axis), (), 0, dims[axis]) for axis in range(len(dims))]
    entries = entries.at[tuple(place)].set(low)
    longest = dims.index(max(dims))
    place[longest] = (place[longest] + 1) % dims[longest]
    return entries.at[tuple(place)].set(largest)


def block_scale(stream_key, shape, cuts, low, largest):
    factor_of = 1.0
    for position, parts in cuts:
        draws = jax.random.uniform(jax.random.fold_in(jax.random.fold_in(stream_key, 6), position), (parts,), jnp.float32, low / len(cuts), largest / len(cuts))
        factor_of = factor_of * jnp.repeat(jnp.exp(draws), shape[position] // parts).reshape((-1,) + (1,) * (len(shape) - 1 - position))
    return factor_of


def scatter_about(own_key, dims, scale, reach, cuts=(), kind=jnp.bfloat16):
    values = scale * jax.random.normal(own_key, dims, jnp.float32)
    if cuts:
        values = values * block_scale(own_key, dims, cuts, -0.22, 0.18)
    return jnp.clip(values, -reach, reach).astype(kind)


def setup_inputs(seed: int = 0, part: int = 0) -> dict:
    key_list = jax.random.split(jax.random.key(seed), 13)
    part_keys = jax.random.split(jax.random.fold_in(key_list[12], part), 13)
    return {
        "tokens": scatter_about(part_keys[0], (N_DEC, N_ENC * TSLOT, TS, TS, D), 1.0, 6.0, ((0, 2), (1, 4))),
        "gain_pre": jnp.clip(jnp.exp(jax.random.uniform(key_list[1], (D,), jnp.float32, math.log(0.5), math.log(2.0))), 0.5, 2.0),
        "w_up": scatter_about(key_list[2], (D, FF), D ** -0.5, 0.15625, ((0, 4), (1, 2))),
        "w_down": scatter_about(key_list[3], (FF, D), FF ** -0.5, 0.125, ((0, 2), (1, 4))),
        "gain_post": jnp.clip(jnp.exp(jax.random.uniform(key_list[4], (D,), jnp.float32, math.log(0.5), math.log(2.0))), 0.5, 2.0),
        "w_neck": scatter_about(key_list[5], (D, C), D ** -0.5, 0.15625),
        "conv_weight": scatter_about(key_list[6], (3, 3, C, C), (9 * C) ** -0.5, 0.125, ((3, 2),)),
        "conv_bias": scatter_about(key_list[7], (C,), 0.5, 3.0, ((0, 2),), jnp.float32),
        "cls_weight": scatter_about(key_list[8], (C, NCLS), C ** -0.5, 0.375, ((0, 2),)),
        "cls_bias": scatter_about(key_list[9], (NCLS,), 1.0, 4.0, (), jnp.float32),
        "tile_table": draw_tile_table(jax.random.fold_in(jax.random.fold_in(key_list[12], part), 71), part),
        "labels": with_ends(jax.random.randint(part_keys[11], (RS, N_ENC, W_ALL), 0, NCLS), jax.random.fold_in(part_keys[11], 1), 0, NCLS - 1).astype(jnp.int32),
    }


norm_eps = 1e-05
blend_sigma = 4.0

def layer_norm(values, scale_vec):
    row_mean = lax.optimization_barrier(jnp.mean(values, axis=-1, keepdims=True))
    centered = values - row_mean
    row_var = lax.optimization_barrier(jnp.mean(centered * centered, axis=-1, keepdims=True))
    return centered * lax.rsqrt(row_var + norm_eps) * scale_vec

def blend_weight(row_pos, col_pos):
    middle = (TS - 1) / 2.0
    spread = ((row_pos - middle) ** 2 + (col_pos - middle) ** 2) / (2.0 * blend_sigma * blend_sigma)
    rounded = lax.optimization_barrier(jnp.exp(-spread).astype(jnp.bfloat16))
    return rounded.astype(jnp.float32)

def encode_band(band_tokens, band_table, gain_pre, w_up, w_down, gain_post, w_neck):
    rows_strip = RS * N_ENC
    stride = TS // 2
    tile_total = 2 * ((rows_strip - TS) // stride + 1)
    slot_ids = jnp.arange(N_ENC * TSLOT, dtype=jnp.int32)
    tile_ids = jnp.arange(tile_total, dtype=jnp.int32)
    matches = (band_table[None, :, 0] == stride * (tile_ids[:, None] // 2)) & (band_table[None, :, 1] == stride * (tile_ids[:, None] % 2))
    chosen = lax.optimization_barrier(jnp.sum(jnp.where(matches, slot_ids[None, :], 0), axis=1)).astype(jnp.int32)
    tile_tokens = jnp.take(band_tokens, chosen, axis=0)
    flat_tok = tile_tokens.reshape(-1, D).astype(jnp.float32)
    normed = layer_norm(flat_tok, gain_pre).astype(jnp.bfloat16)
    hidden = jax.nn.gelu(jnp.dot(normed, w_up, preferred_element_type=jnp.float32), approximate=False).astype(jnp.bfloat16)
    block_size = FF // N_MP
    branch = jnp.zeros(flat_tok.shape, jnp.float32)
    for member in range(N_MP):
        partial_value = jnp.dot(hidden[:, member * block_size:(member + 1) * block_size], w_down[member * block_size:(member + 1) * block_size], preferred_element_type=jnp.float32)
        branch = branch + lax.optimization_barrier(partial_value.astype(jnp.bfloat16)).astype(jnp.float32)
    features = layer_norm(flat_tok + branch, gain_post).astype(jnp.bfloat16)
    tile_maps = jnp.dot(features, w_neck, preferred_element_type=jnp.float32).astype(jnp.bfloat16).reshape(tile_total, TS, TS, C)
    grid_pos = jnp.arange(TS).astype(jnp.float32)
    weights = blend_weight(grid_pos[:, None], grid_pos[None, :])
    numer = jnp.zeros((rows_strip, BAND, C), jnp.float32)
    denom = jnp.zeros((rows_strip, BAND), jnp.float32)
    for tile_num in range(tile_total):
        row_top = stride * (tile_num // 2)
        col_left = stride * (tile_num % 2)
        numer = numer.at[row_top:row_top + TS, col_left:col_left + TS].add(tile_maps[tile_num].astype(jnp.float32) * weights[:, :, None])
        denom = denom.at[row_top:row_top + TS, col_left:col_left + TS].add(weights)
    return (numer / denom[:, :, None]).astype(jnp.bfloat16)

def reference(tokens, gain_pre, w_up, w_down, gain_post, w_neck, conv_weight, conv_bias, cls_weight, cls_bias, tile_table, labels):
    rows_strip = RS * N_ENC
    width_all = N_DEC * BAND

    def one_band(pair):
        return encode_band(pair[0], pair[1], gain_pre, w_up, w_down, gain_post, w_neck)
    banded = lax.map(one_band, (tokens, tile_table))
    merged = jnp.transpose(banded, (1, 0, 2, 3)).reshape(rows_strip, width_all, C)
    padded = jnp.pad(merged, ((1, 1), (1, 1), (0, 0)))
    conv_sum = jnp.zeros((rows_strip * width_all, C), jnp.float32)
    for row_off in range(3):
        for col_off in range(3):
            window = padded[row_off:row_off + rows_strip, col_off:col_off + width_all].reshape(-1, C)
            conv_sum = conv_sum + jnp.dot(window, conv_weight[row_off, col_off], preferred_element_type=jnp.float32)
    activ = jax.nn.relu(conv_sum + conv_bias).astype(jnp.bfloat16)
    logits = jnp.dot(activ, cls_weight, preferred_element_type=jnp.float32) + cls_bias
    logits = logits.reshape(RS, N_ENC, width_all, NCLS)
    classes = jnp.arange(NCLS, dtype=jnp.int32)
    picked = lax.optimization_barrier(jnp.sum(jnp.where(labels[..., None] == classes, logits, 0.0), axis=-1))
    nll = jnp.log(lax.optimization_barrier(jnp.sum(jnp.exp(logits), axis=-1))) - picked
    return (logits, nll)
```

```python
import functools

import jax
import jax.numpy as jnp
from jax import lax
from jax.experimental import pallas as pl
from jax.experimental.pallas import tpu as pltpu
from jax.sharding import PartitionSpec as P

TS = 16
EDGE = 8
PAD = 8

norm_eps = 1e-05
blend_sigma = 4.0

F32 = jnp.float32
BF16 = jnp.bfloat16


VMEM = pl.BlockSpec(memory_space=pltpu.VMEM)
SMEM = pl.BlockSpec(memory_space=pltpu.SMEM)
ANY = pl.BlockSpec(memory_space=pl.ANY)
PARAMS = pltpu.CompilerParams(vmem_limit_bytes=56 * 1024 * 1024)


def flip(value, axis):
    size = lax.axis_size(axis)
    return lax.ppermute(value, axis, [(i, i ^ 1) for i in range(size)])


def fold_order(size):
    return [0] + list(range(1, size, 2)) + list(range(size - 2 + size % 2, 0, -2))


def ring(value, axis):
    size = lax.axis_size(axis)
    order = fold_order(size)
    return lax.ppermute(
        value, axis, [(order[i], order[(i + 1) % size]) for i in range(size)]
    )


def fold_plane(z, step, size):
    place = jnp.where(z % 2 == 1, (z + 1) // 2, jnp.where(z == 0, 0, size - z // 2))
    place = (place - step + size) % size
    return jnp.where(
        place == 0, 0, jnp.where(place <= size // 2, 2 * place - 1, 2 * (size - place))
    )


def gather_pieces(quarter, far, turn, name):
    size = lax.axis_size("enc")
    pieces = []
    moving = quarter
    for step in range(1, size):
        with jax.named_scope(f"{name}z{step}"):
            moving = ring(moving, "enc")
        if far is None:
            pieces.append(moving)
            continue
        with jax.named_scope(f"{name}x{step}"):
            across = flip(moving, "dec")
        with jax.named_scope(f"{name}y{step}"):
            along = flip(moving, "groups")
        with jax.named_scope(f"{name}g{step}"):
            if step == 1:
                both = ring(far, "enc")
            elif (step + turn) % 2:
                both = flip(along, "dec")
            else:
                both = flip(across, "groups")
        pieces += [moving, across, along, both]
    return pieces


def spread_of(rows):
    return 4 if rows % 64 == 0 else 1


def assemble(where, own, pieces, target, sems, enc_size):
    z, quarter = where[0], where[2]
    rows = own.shape[0]
    kinds = spread_of(rows)
    part = rows // kinds
    copies = [
        pltpu.make_async_copy(
            own, target.at[pl.ds(pl.multiple_of(z * rows, rows), rows)], sems.at[0]
        )
    ]
    for step in range(1, enc_size):
        plane = fold_plane(z, step, enc_size)
        for kind in range(kinds):
            index = kinds * (step - 1) + kind
            start = plane * rows
            if kinds > 1:
                start = start + (quarter ^ kind) * part
            copies.append(
                pltpu.make_async_copy(
                    pieces[index],
                    target.at[pl.ds(pl.multiple_of(start, part), part)],
                    sems.at[index + 1],
                )
            )
    for copy in copies:
        copy.start()
    for copy in copies:
        copy.wait()


def norm_kernel(tok_ref, gain_ref, out_ref):
    values = tok_ref[...].reshape(out_ref.shape).astype(F32)
    out_ref[...] = normalize(values, gain_ref[...]).astype(BF16)


def normalize(values, gain):
    mean = jnp.mean(values, axis=-1, keepdims=True)
    centered = values - mean
    var = jnp.mean(centered * centered, axis=-1, keepdims=True)
    return centered * lax.rsqrt(var + norm_eps) * gain


def up_kernel(enc_size, where, normed_ref, own, *rest):
    pieces, (out_ref, weight, sems) = rest[:-3], rest[-3:]

    @pl.when(pl.program_id(0) == 0)
    def _():
        assemble(where, own, pieces, weight, sems, enc_size)

    pre = jnp.dot(normed_ref[...], weight[...], preferred_element_type=F32)
    out_ref[...] = (0.5 * pre * (1.0 + lax.erf(pre * (0.5**0.5)))).astype(BF16)


def down_kernel(enc_size, where, hidden_ref, own, *rest):
    pieces, (out_ref, weight, sems) = rest[:-3], rest[-3:]

    @pl.when(pl.program_id(0) == 0)
    def _():
        assemble(where, own, pieces, weight, sems, enc_size)

    out_ref[...] = lax.dot_general(
        hidden_ref[...], weight[...], (((1,), (1,)), ((), ())), preferred_element_type=F32
    ).astype(BF16)


def project_kernel(
    enc_size, where, table, tok_ref, own_ref, other_ref, gain_ref, neck_ref, *rest
):
    outs, (acc, den) = rest[:-2], rest[-2:]
    z, m = where[0], where[1]
    slot = pl.program_id(0)
    slots = pl.num_programs(0)
    half = TS // 2
    channels = neck_ref.shape[1]
    shape = (half, TS, den.shape[2])
    row = (2 * lax.broadcasted_iota(jnp.int32, shape, 0) + m).astype(F32)
    col = lax.broadcasted_iota(jnp.int32, shape, 1).astype(F32)
    middle = (TS - 1) / 2.0
    spread = ((row - middle) ** 2 + (col - middle) ** 2) / (2.0 * blend_sigma * blend_sigma)
    weight = jnp.exp(-spread).astype(BF16).astype(F32)

    @pl.when(slot == 0)
    def _():
        acc[...] = jnp.zeros_like(acc)
        den[...] = jnp.zeros_like(den)
        den[0] = jnp.ones_like(den[0])
        den[den.shape[0] - 1] = jnp.ones_like(den[0])

        def add_entry(entry, carry):
            top, left = table[2 * entry], table[2 * entry + 1]

            @pl.when(top >= 0)
            def _():
                rows = pl.ds(top // 2 + 1, half)
                cols = pl.ds(pl.multiple_of(left, 8), TS)
                den[rows, cols, :] = den[rows, cols, :] + weight

            return carry

        lax.fori_loop(0, slots * enc_size, add_entry, 0)

    branch = own_ref[...].astype(F32) + other_ref[...].astype(F32)
    values = tok_ref[...].reshape(branch.shape).astype(F32) + branch
    features = normalize(values, gain_ref[...]).astype(BF16)
    maps = jnp.dot(features, neck_ref[...], preferred_element_type=F32).astype(BF16)
    maps = maps.astype(F32).reshape(half, TS, channels)
    entry = z * slots + slot
    top, left = table[2 * entry], table[2 * entry + 1]

    @pl.when(top >= 0)
    def _():
        rows = pl.ds(top // 2 + 1, half)
        cols = pl.ds(pl.multiple_of(left, 8), TS)
        wide = jnp.concatenate([weight] * (channels // weight.shape[2]), axis=2)
        acc[rows, cols, :] = acc[rows, cols, :] + maps * wide

    @pl.when(slot == slots - 1)
    def _():
        for step, out in enumerate(outs):
            start = (z ^ step) * (half // 2) + (1 - m)
            rows = pl.ds(start, half // 2 + 1)
            below = den[rows]
            below = jnp.concatenate([below] * (channels // below.shape[2]), axis=2)
            out[...] = (acc[rows] / below).reshape(out.shape).astype(BF16)


def merge_kernel(sides, where, *rest):
    parts, outs = rest[: len(rest) - 1 - sides], rest[len(rest) - 1 - sides :]
    total = parts[0][...].astype(F32)
    for part in parts[1:]:
        total = total + part[...].astype(F32)
    outs[0][...] = total.astype(BF16)
    rows = TS // 4 + 1
    grid = total.reshape(rows, total.shape[0] // rows, total.shape[1])
    last = grid.shape[1] - 1
    left, right = grid[:, 0, :], grid[:, last, :]
    if sides == 1:
        outs[1][:rows] = jnp.where(where[3] % 2 == 0, right, left).astype(BF16)
    else:
        outs[1][:rows] = right.astype(BF16)
        outs[2][:rows] = left.astype(BF16)


def conv_kernel(
    enc_size, sides, band, where, own, other, conv_w, bias_own, bias_other, cls_own,
    cls_other, cls_bias, *rest
):
    edges, outs, (grid, logit) = rest[: 2 * sides], rest[2 * sides : -2], rest[-2:]
    z, m, d = where[0], where[1], where[3]
    rows = own.shape[0] // band
    channels = own.shape[1]
    half = conv_w.shape[3] // 2
    grid[...] = jnp.zeros_like(grid)
    for who, (body, lane) in enumerate(((own, 1 - m), (other, m))):
        grid[:, lane, PAD : PAD + band, :] = body[...].astype(F32).reshape(rows, band, channels)
        for side in range(sides):
            edge = edges[2 * side + who][...].astype(F32)[:rows].reshape(rows, 1, channels)
            if sides == 2:
                place = PAD - 1 if side == 0 else PAD + band
                grid[:, lane, place : place + 1, :] = edge
            else:

                @pl.when(d % 2 == 1)
                def _():
                    grid[:, lane, PAD - 1 : PAD, :] = edge

                @pl.when(d % 2 == 0)
                def _():
                    grid[:, lane, PAD + band : PAD + band + 1, :] = edge

    count = 2 * rows - 2
    total = jnp.zeros((count * band, 2 * half), F32)
    for col_off in range(3):
        start = PAD - 1 + col_off
        window = grid[:, :, start : start + band, :].reshape(2 * rows, band, channels)
        for row_off in range(3):
            lhs = window[row_off : row_off + count].reshape(count * band, channels)
            total = total + jnp.dot(
                lhs.astype(BF16), conv_w[row_off, col_off], preferred_element_type=F32
            )
    sums = []
    for which, (bias, cls) in enumerate(((bias_own, cls_own), (bias_other, cls_other))):
        activ = total[:, which * half : (which + 1) * half] + bias[...]
        activ = jnp.maximum(activ, 0.0).astype(BF16)
        sums.append(
            lax.dot_general(
                cls[...], activ, (((1,), (1,)), ((), ())), preferred_element_type=F32
            )
        )
    result = sums[0] + sums[1] + cls_bias[...]
    for row in range(count):
        logit[row] = result[:, row * band : (row + 1) * band]
    for step, out in enumerate(outs):
        for turn in range(out.shape[0]):
            place = row_for(z ^ step, z, enc_size, count) + turn * enc_size
            out[turn] = logit[jnp.minimum(place, count - 1)]


def row_for(receiver, owner, enc_size, count):
    return (receiver + enc_size * count - owner * count) % enc_size


def loss_kernel(enc_size, where, labels, *rest):
    parts, (logits_ref, nll_ref) = rest[:-2], rest[-2:]
    z = where[0]
    count = labels.shape[0]
    for step, part in enumerate(parts):
        owner = z ^ step
        for turn in range(part.shape[0]):
            place = row_for(z, owner, enc_size, count) + turn * enc_size
            logits = part[turn]
            row = (owner * count + place) // enc_size

            @pl.when(place < count)
            def _():
                logits_ref[row, :, 0, :] = logits
                label = labels[row]
                classes = lax.broadcasted_iota(jnp.int32, logits.shape, 0)
                picked = jnp.sum(
                    jnp.where(label == classes, logits, 0.0), axis=0, keepdims=True
                )
                nll_ref[row] = jnp.log(jnp.sum(jnp.exp(logits), axis=0, keepdims=True)) - picked


def body(
    tokens,
    gain_pre,
    w_up,
    w_down,
    gain_post,
    w_neck,
    conv_weight,
    conv_bias,
    cls_weight,
    cls_bias,
    tile_table,
    labels,
):
    enc_size = lax.axis_size("enc")
    dec_size = lax.axis_size("dec")
    slots, width = tokens.shape[1], tokens.shape[4]
    ff = w_up.shape[1]
    channels = w_neck.shape[1]
    rows_local, band = labels.shape[0], labels.shape[2]
    classes = cls_weight.shape[1]
    half = TS // 2
    z, m, d = lax.axis_index("enc"), lax.axis_index("mp"), lax.axis_index("dec")
    quarter = (lax.axis_index("groups") % 2) * 2 + d % 2
    where = jnp.stack([z, m, quarter, d]).astype(jnp.int32)

    down_t = w_down.T
    kinds = spread_of(w_up.shape[0])
    part = w_up.shape[0] // kinds
    cut = lambda value, index: lax.dynamic_slice_in_dim(value, index * part, part, 0)
    if kinds == 1:
        up_pieces = gather_pieces(w_up, None, 0, "u")
        down_pieces = gather_pieces(down_t, None, 1, "d")
    else:
        up_pieces = gather_pieces(cut(w_up, quarter), cut(w_up, quarter ^ 3), 0, "u")
        down_pieces = gather_pieces(cut(down_t, quarter), cut(down_t, quarter ^ 3), 1, "d")
    conv_other = flip(conv_weight, "mp")
    cls_t = cls_weight.T
    cls_other = flip(cls_t, "mp")
    bias = conv_bias.reshape(1, -1)
    bias_other = flip(bias, "mp")
    conv_full = jnp.concatenate([conv_weight, conv_other], axis=3)

    tok = tokens.reshape(slots, half, 2, TS, width)
    per_slot = half * TS
    count = slots * per_slot
    normed = pl.pallas_call(
        norm_kernel,
        grid=(2, slots),
        in_specs=[
            pl.BlockSpec((1, half, 1, TS, width), lambda p, s: (s, 0, p, 0, 0)),
            pl.BlockSpec((1, width), lambda p, s: (0, 0)),
        ],
        out_specs=pl.BlockSpec((per_slot, width), lambda p, s: (p * slots + s, 0)),
        out_shape=jax.ShapeDtypeStruct((2 * count, width), BF16),
        compiler_params=PARAMS,
        name="norm",
    )(tok, gain_pre.reshape(1, -1))

    pieces_count = kinds * (enc_size - 1)
    weight_scratch = [
        pltpu.VMEM((w_up.shape[0] * enc_size, ff), BF16),
        pltpu.SemaphoreType.DMA((pieces_count + 1,)),
    ]
    block = 256
    hidden = pl.pallas_call(
        functools.partial(up_kernel, enc_size),
        grid_spec=pltpu.PrefetchScalarGridSpec(
            num_scalar_prefetch=1,
            grid=(2 * count // block,),
            in_specs=[pl.BlockSpec((block, width), lambda i, w: (i, 0))]
            + [ANY] * (pieces_count + 1),
            out_specs=pl.BlockSpec((block, ff), lambda i, w: (i, 0)),
            scratch_shapes=weight_scratch,
        ),
        out_shape=jax.ShapeDtypeStruct((2 * count, ff), BF16),
        compiler_params=PARAMS,
        name="up",
    )(where, normed, w_up, *up_pieces)

    def down(which):
        chosen = (lambda w: w[1]) if which == 0 else (lambda w: 1 - w[1])
        return pl.pallas_call(
            functools.partial(down_kernel, enc_size),
            grid_spec=pltpu.PrefetchScalarGridSpec(
                num_scalar_prefetch=1,
                grid=(count // block,),
                in_specs=[
                    pl.BlockSpec(
                        (block, ff), lambda i, w: (chosen(w) * (count // block) + i, 0)
                    )
                ]
                + [ANY] * (pieces_count + 1),
                out_specs=pl.BlockSpec((block, width), lambda i, w: (i, 0)),
                scratch_shapes=weight_scratch,
            ),
            out_shape=jax.ShapeDtypeStruct((count, width), BF16),
            compiler_params=PARAMS,
            name="down_own" if which == 0 else "down_other",
        )(where, hidden, down_t, *down_pieces)

    received = flip(down(1), "mp")
    branch = down(0)

    table = tile_table[0].reshape(-1)
    strip_rows = rows_local * enc_size // 2 + 2
    out_rows = rows_local // 2 + 1
    messages = pl.pallas_call(
        functools.partial(project_kernel, enc_size),
        grid_spec=pltpu.PrefetchScalarGridSpec(
            num_scalar_prefetch=2,
            grid=(slots,),
            in_specs=[
                pl.BlockSpec(
                    (1, half, 1, TS, width), lambda s, w, t: (s, 0, w[1], 0, 0)
                ),
                pl.BlockSpec((per_slot, width), lambda s, w, t: (s, 0)),
                pl.BlockSpec((per_slot, width), lambda s, w, t: (s, 0)),
                pl.BlockSpec((1, width), lambda s, w, t: (0, 0)),
                pl.BlockSpec((width, channels), lambda s, w, t: (0, 0)),
            ],
            out_specs=[
                pl.BlockSpec((out_rows * band, channels), lambda s, w, t: (0, 0))
            ]
            * enc_size,
            scratch_shapes=[
                pltpu.VMEM((strip_rows, band, channels), F32),
                pltpu.VMEM((strip_rows, band, 128), F32),
            ],
        ),
        out_shape=[jax.ShapeDtypeStruct((out_rows * band, channels), BF16)] * enc_size,
        compiler_params=PARAMS,
        name="project",
    )(where, table, tok, branch, received, gain_post.reshape(1, -1), w_neck)
    swap = lambda value, step: lax.ppermute(
        value, "enc", [(i, i ^ step) for i in range(enc_size)]
    )
    parts = [messages[0]] + [swap(messages[k], k) for k in range(1, enc_size)]

    sides = 1 if dec_size == 2 else 2
    edge_shape = jax.ShapeDtypeStruct((EDGE, channels), BF16)
    strip, *edges = pl.pallas_call(
        functools.partial(merge_kernel, sides),
        in_specs=[SMEM] + [VMEM] * enc_size,
        out_specs=[VMEM] * (1 + sides),
        out_shape=[jax.ShapeDtypeStruct((out_rows * band, channels), BF16)]
        + [edge_shape] * sides,
        compiler_params=PARAMS,
        name="merge",
    )(where, *parts)
    strip_other = flip(strip, "mp")
    flat = lambda dd, mm: dd * 2 + mm
    halo = []
    for side in range(sides):
        for cross in range(2):
            if sides == 1:
                pairs = [
                    (flat(i, c), flat(i ^ 1, c ^ cross)) for i in range(dec_size) for c in range(2)
                ]
            else:
                by = 1 if side == 0 else -1
                pairs = [
                    (flat(i, c), flat(i + by, c ^ cross))
                    for i in range(dec_size)
                    for c in range(2)
                    if 0 <= i + by < dec_size
                ]
            halo.append(lax.ppermute(edges[side], ("dec", "mp"), pairs))
    turns = max(1, rows_local // enc_size)
    logits_parts = pl.pallas_call(
        functools.partial(conv_kernel, enc_size, sides, band),
        in_specs=[SMEM] + [VMEM] * (8 + 2 * sides),
        out_specs=[VMEM] * enc_size,
        out_shape=[jax.ShapeDtypeStruct((turns, classes, band), F32)] * enc_size,
        scratch_shapes=[
            pltpu.VMEM((out_rows, 2, PAD + band + PAD, channels), F32),
            pltpu.VMEM((rows_local, classes, band), F32),
        ],
        compiler_params=PARAMS,
        name="conv",
    )(
        where, strip, strip_other, conv_full, bias, bias_other, cls_t, cls_other,
        cls_bias.reshape(-1, 1), *halo,
    )
    dealt = [logits_parts[0]] + [swap(logits_parts[k], k) for k in range(1, enc_size)]
    logits, nll = pl.pallas_call(
        functools.partial(loss_kernel, enc_size),
        in_specs=[SMEM] + [VMEM] * (1 + enc_size),
        out_specs=[VMEM] * 2,
        out_shape=[
            jax.ShapeDtypeStruct((rows_local, classes, 1, band), F32),
            jax.ShapeDtypeStruct((rows_local, 1, band), F32),
        ],
        compiler_params=PARAMS,
        name="loss",
    )(where, labels, *dealt)
    return (jnp.transpose(logits, (0, 2, 3, 1)), nll)


def solution(mesh):
    in_specs = (
        P(("groups", "dec"), "enc", None, None, None),
        P(),
        P("enc", "mp"),
        P("mp", "enc"),
        P(),
        P(),
        P(None, None, None, "mp"),
        P("mp"),
        P("mp", None),
        P(),
        P(("groups", "dec"), None, None),
        P(None, "enc", ("groups", "dec")),
    )
    out_specs = (P(None, "enc", ("groups", "dec"), None), P(None, "enc", ("groups", "dec")))
    return jax.shard_map(body, mesh=mesh, in_specs=in_specs, out_specs=out_specs, check_vma=False)
```

```python
import functools

import jax
import jax.numpy as jnp
from jax import lax
from jax.experimental import pallas as pl
from jax.experimental.pallas import tpu as pltpu
from jax.sharding import PartitionSpec as P


TS = 16
EDGE = 8
PAD = 8

norm_eps = 1e-05
blend_sigma = 4.0

F32 = jnp.float32
BF16 = jnp.bfloat16


VMEM = pl.BlockSpec(memory_space=pltpu.VMEM)
SMEM = pl.BlockSpec(memory_space=pltpu.SMEM)
ANY = pl.BlockSpec(memory_space=pl.ANY)
PARAMS = pltpu.CompilerParams(vmem_limit_bytes=24 * 1024 * 1024)


def near(value):
    return pltpu.with_memory_space_constraint(value, pltpu.VMEM)


def flip(value, axis):
    size = lax.axis_size(axis)
    return lax.ppermute(value, axis, [(i, i ^ 1) for i in range(size)])


def fold_order(size):
    return [0] + list(range(1, size, 2)) + list(range(size - 2 + size % 2, 0, -2))


def ring(value, axis):
    size = lax.axis_size(axis)
    order = fold_order(size)
    return lax.ppermute(
        value, axis, [(order[i], order[(i + 1) % size]) for i in range(size)]
    )


def fold_plane(z, step, size):
    place = jnp.where(z % 2 == 1, (z + 1) // 2, jnp.where(z == 0, 0, size - z // 2))
    place = (place - step + size) % size
    return jnp.where(
        place == 0, 0, jnp.where(place <= size // 2, 2 * place - 1, 2 * (size - place))
    )


def gather_pieces(quarter, far, turn):
    size = lax.axis_size("enc")
    pieces = []
    moving = quarter
    for step in range(1, size):
        moving = ring(moving, "enc")
        if far is None:
            pieces.append(moving)
            continue
        across = flip(moving, "dec")
        along = flip(moving, "groups")
        if step == 1:
            both = ring(far, "enc")
        elif (step + turn) % 2:
            both = flip(along, "dec")
        else:
            both = flip(across, "groups")
        pieces += [moving, across, along, both]
    return pieces


def spread_of(rows):
    return 4 if rows % 64 == 0 else 1


def cut_kernel(parts, where, up, down, *rest):
    outs, sems = rest[:-1], rest[-1]
    quarter = where[2]
    copies = []
    for index, out in enumerate(outs):
        rows = out.shape[0]
        source = (up, down)[index // (len(outs) // 2)]
        start = (quarter ^ (3 * (index % 2))) * rows if parts > 1 else 0
        copies.append(
            pltpu.make_async_copy(
                source.at[pl.ds(pl.multiple_of(start, rows), rows)], out, sems.at[index]
            )
        )
    for copy in copies:
        copy.start()
    for copy in copies:
        copy.wait()


def assemble_kernel(enc_size, where, own, *rest):
    pieces, (target, sem) = rest[:-2], rest[-2:]
    z, quarter = where[0], where[2]
    rows = own.shape[0]
    kinds = spread_of(rows)
    part = rows // kinds
    copy = pltpu.make_async_copy(
        own, target.at[pl.ds(pl.multiple_of(z * rows, rows), rows)], sem
    )
    copy.start()
    for step in range(1, enc_size):
        plane = fold_plane(z, step, enc_size)
        for kind in range(kinds):
            start = plane * rows
            if kinds > 1:
                start = start + (quarter ^ kind) * part
            rows_at = pl.ds(pl.multiple_of(start, part), part)
            target[rows_at, :] = pieces[kinds * (step - 1) + kind][...]
    copy.wait()


def norm_kernel(where, tok_ref, gain_ref, out_ref):
    values = tok_ref[...].reshape(out_ref.shape).astype(F32)
    out_ref[...] = normalize(values, gain_ref[...]).astype(BF16)


def normalize(values, gain):
    mean = jnp.mean(values, axis=-1, keepdims=True)
    centered = values - mean
    var = jnp.mean(centered * centered, axis=-1, keepdims=True)
    return centered * lax.rsqrt(var + norm_eps) * gain


def up_kernel(normed, weight, out):
    pre = jnp.dot(normed[...], weight[...], preferred_element_type=F32)
    out[...] = (0.5 * pre * (1.0 + lax.erf(pre * (0.5**0.5)))).astype(BF16)


def down_kernel(hidden, weight, out):
    out[...] = lax.dot_general(
        hidden[...], weight[...], (((1,), (1,)), ((), ())), preferred_element_type=F32
    ).astype(BF16)


def project_kernel(
    enc_size, where, table, tok_ref, own_ref, other_ref, gain_ref, neck_ref, *rest
):
    outs, (acc, den) = rest[:-2], rest[-2:]
    z, m = where[0], where[1]
    slot = pl.program_id(0)
    slots = pl.num_programs(0)
    half = TS // 2
    channels = neck_ref.shape[1]
    shape = (half, TS, den.shape[2])
    row = (2 * lax.broadcasted_iota(jnp.int32, shape, 0) + m).astype(F32)
    col = lax.broadcasted_iota(jnp.int32, shape, 1).astype(F32)
    middle = (TS - 1) / 2.0
    spread = ((row - middle) ** 2 + (col - middle) ** 2) / (2.0 * blend_sigma * blend_sigma)
    weight = jnp.exp(-spread).astype(BF16).astype(F32)

    @pl.when(slot == 0)
    def _():
        acc[...] = jnp.zeros_like(acc)
        den[...] = jnp.zeros_like(den)
        den[0] = jnp.ones_like(den[0])
        den[den.shape[0] - 1] = jnp.ones_like(den[0])

        def add_entry(entry, carry):
            top, left = table[2 * entry], table[2 * entry + 1]

            @pl.when(top >= 0)
            def _():
                rows = pl.ds(top // 2 + 1, half)
                cols = pl.ds(pl.multiple_of(left, 8), TS)
                den[rows, cols, :] = den[rows, cols, :] + weight

            return carry

        lax.fori_loop(0, slots * enc_size, add_entry, 0)

    branch = own_ref[...].astype(F32) + other_ref[...].astype(F32)
    values = tok_ref[...].reshape(branch.shape).astype(F32) + branch
    features = normalize(values, gain_ref[...]).astype(BF16)
    maps = jnp.dot(features, neck_ref[...], preferred_element_type=F32).astype(BF16)
    maps = maps.astype(F32).reshape(half, TS, channels)
    entry = z * slots + slot
    top, left = table[2 * entry], table[2 * entry + 1]

    @pl.when(top >= 0)
    def _():
        rows = pl.ds(top // 2 + 1, half)
        cols = pl.ds(pl.multiple_of(left, 8), TS)
        wide = jnp.concatenate([weight] * (channels // weight.shape[2]), axis=2)
        acc[rows, cols, :] = acc[rows, cols, :] + maps * wide

    @pl.when(slot == slots - 1)
    def _():
        for step, out in enumerate(outs):
            start = (z ^ step) * (half // 2) + (1 - m)
            rows = pl.ds(start, half // 2 + 1)
            below = den[rows]
            below = jnp.concatenate([below] * (channels // below.shape[2]), axis=2)
            out[...] = (acc[rows] / below).reshape(out.shape).astype(BF16)


def merge_kernel(sides, where, *rest):
    parts, outs = rest[: len(rest) - 1 - sides], rest[len(rest) - 1 - sides :]
    total = parts[0][...].astype(F32)
    for part in parts[1:]:
        total = total + part[...].astype(F32)
    outs[0][...] = total.astype(BF16)
    rows = TS // 4 + 1
    grid = total.reshape(rows, total.shape[0] // rows, total.shape[1])
    last = grid.shape[1] - 1
    left, right = grid[:, 0, :], grid[:, last, :]
    if sides == 1:
        outs[1][:rows] = jnp.where(where[3] % 2 == 0, right, left).astype(BF16)
    else:
        outs[1][:rows] = right.astype(BF16)
        outs[2][:rows] = left.astype(BF16)


def conv_kernel(
    enc_size, sides, band, where, own, other, conv_own, conv_other, bias_own, bias_other,
    cls_own, cls_other, cls_bias, *rest
):
    edges, outs, (grid, logit) = rest[: 2 * sides], rest[2 * sides : -2], rest[-2:]
    z, m, d = where[0], where[1], where[3]
    rows = own.shape[0] // band
    channels = own.shape[1]
    half = conv_own.shape[3]
    grid[...] = jnp.zeros_like(grid)
    for who, (body, lane) in enumerate(((own, 1 - m), (other, m))):
        grid[:, lane, PAD : PAD + band, :] = body[...].astype(F32).reshape(rows, band, channels)
        for side in range(sides):
            edge = edges[2 * side + who][...].astype(F32)[:rows].reshape(rows, 1, channels)
            if sides == 2:
                place = PAD - 1 if side == 0 else PAD + band
                grid[:, lane, place : place + 1, :] = edge
            else:

                @pl.when(d % 2 == 1)
                def _():
                    grid[:, lane, PAD - 1 : PAD, :] = edge

                @pl.when(d % 2 == 0)
                def _():
                    grid[:, lane, PAD + band : PAD + band + 1, :] = edge

    count = 2 * rows - 2
    total = jnp.zeros((count * band, 2 * half), F32)
    for col_off in range(3):
        start = PAD - 1 + col_off
        window = grid[:, :, start : start + band, :].reshape(2 * rows, band, channels)
        for row_off in range(3):
            lhs = window[row_off : row_off + count].reshape(count * band, channels)
            both = (conv_own[row_off, col_off], conv_other[row_off, col_off])
            total = total + jnp.dot(
                lhs.astype(BF16), jnp.concatenate(both, axis=1), preferred_element_type=F32
            )
    sums = []
    for which, (bias, cls) in enumerate(((bias_own, cls_own), (bias_other, cls_other))):
        activ = total[:, which * half : (which + 1) * half] + bias[...]
        activ = jnp.maximum(activ, 0.0).astype(BF16)
        sums.append(
            lax.dot_general(
                cls[...], activ, (((1,), (1,)), ((), ())), preferred_element_type=F32
            )
        )
    result = sums[0] + sums[1] + cls_bias[...]
    for row in range(count):
        logit[row] = result[:, row * band : (row + 1) * band]
    for step, out in enumerate(outs):
        for turn in range(out.shape[0]):
            place = row_for(z ^ step, z, enc_size, count) + turn * enc_size
            out[turn] = logit[jnp.minimum(place, count - 1)]


def row_for(receiver, owner, enc_size, count):
    return (receiver + enc_size * count - owner * count) % enc_size


def loss_kernel(enc_size, where, labels, *rest):
    parts, (logits_ref, nll_ref) = rest[:-2], rest[-2:]
    z = where[0]
    count = labels.shape[0]
    for step, part in enumerate(parts):
        owner = z ^ step
        for turn in range(part.shape[0]):
            place = row_for(z, owner, enc_size, count) + turn * enc_size
            logits = part[turn]
            row = (owner * count + place) // enc_size

            @pl.when(place < count)
            def _():
                logits_ref[row, :, 0, :] = logits
                label = labels[row]
                classes = lax.broadcasted_iota(jnp.int32, logits.shape, 0)
                picked = jnp.sum(
                    jnp.where(label == classes, logits, 0.0), axis=0, keepdims=True
                )
                nll_ref[row] = jnp.log(jnp.sum(jnp.exp(logits), axis=0, keepdims=True)) - picked


def segment(
    tokens,
    gain_pre,
    w_up,
    w_down,
    gain_post,
    w_neck,
    conv_weight,
    conv_bias,
    cls_weight,
    cls_bias,
    tile_table,
    labels,
):
    enc_size = lax.axis_size("enc")
    dec_size = lax.axis_size("dec")
    slots, width = tokens.shape[1], tokens.shape[4]
    ff = w_up.shape[1]
    channels = w_neck.shape[1]
    rows_local, band = labels.shape[0], labels.shape[2]
    classes = cls_weight.shape[1]
    half = TS // 2
    z, m, d = lax.axis_index("enc"), lax.axis_index("mp"), lax.axis_index("dec")
    quarter = (lax.axis_index("groups") % 2) * 2 + d % 2
    where = jnp.stack([z, m, quarter, d]).astype(jnp.int32)

    down_t = w_down.T
    kinds = spread_of(w_up.shape[0])
    part = w_up.shape[0] // kinds
    piece = jax.ShapeDtypeStruct((part, ff), BF16)
    cuts = pl.pallas_call(
        functools.partial(cut_kernel, kinds),
        in_specs=[SMEM, ANY, ANY],
        out_specs=[VMEM] * (4 if kinds > 1 else 2),
        out_shape=[piece] * (4 if kinds > 1 else 2),
        scratch_shapes=[pltpu.SemaphoreType.DMA((4,))],
        compiler_params=PARAMS,
        name="cut",
    )(where, w_up, down_t)
    if kinds == 1:
        cuts = [cuts[0], None, cuts[1], None]
    up_pieces = gather_pieces(cuts[0], cuts[1], 0)
    down_pieces = gather_pieces(cuts[2], cuts[3], 1)
    conv_other = flip(conv_weight, "mp")
    cls_t = cls_weight.T
    cls_other = flip(cls_t, "mp")
    bias = conv_bias.reshape(1, -1)
    bias_other = flip(bias, "mp")

    tok = tokens.reshape(slots, half, 2, TS, width)
    per_slot = half * TS
    count = slots * per_slot
    halves = {"own": lambda w: w[1], "other": lambda w: 1 - w[1]}

    def norm(which):
        return pl.pallas_call(
            norm_kernel,
            grid_spec=pltpu.PrefetchScalarGridSpec(
                num_scalar_prefetch=1,
                grid=(slots // 2,),
                in_specs=[
                    pl.BlockSpec(
                        (2, half, 1, TS, width),
                        lambda s, w: (s, 0, halves[which](w), 0, 0),
                    ),
                    pl.BlockSpec((1, width), lambda s, w: (0, 0)),
                ],
                out_specs=pl.BlockSpec((2 * per_slot, width), lambda s, w: (s, 0)),
            ),
            out_shape=jax.ShapeDtypeStruct((count, width), BF16),
            compiler_params=PARAMS,
        )(where, tok, gain_pre.reshape(1, -1))

    def assembled(shard, pieces):
        return pl.pallas_call(
            functools.partial(assemble_kernel, enc_size),
            in_specs=[SMEM, ANY] + [VMEM] * len(pieces),
            out_specs=VMEM,
            out_shape=jax.ShapeDtypeStruct((shard.shape[0] * enc_size, ff), BF16),
            scratch_shapes=[pltpu.SemaphoreType.DMA],
            compiler_params=PARAMS,
        )(where, shard, *[near(value) for value in pieces])

    block = 256

    def matmul(kernel, value, weight, columns):
        return pl.pallas_call(
            kernel,
            grid=(count // block,),
            in_specs=[pl.BlockSpec((block, value.shape[1]), lambda i: (i, 0)), VMEM],
            out_specs=pl.BlockSpec((block, columns), lambda i: (i, 0)),
            out_shape=jax.ShapeDtypeStruct((count, columns), BF16),
            compiler_params=PARAMS,
        )(value, near(weight))

    normed_other = norm("other")
    normed_own = norm("own")
    up_weight = assembled(w_up, up_pieces)
    hidden_other = matmul(up_kernel, normed_other, up_weight, ff)
    hidden_own = matmul(up_kernel, normed_own, up_weight, ff)
    down_weight = assembled(down_t, down_pieces)
    part_other = matmul(down_kernel, hidden_other, down_weight, width)
    received = flip(part_other, "mp")
    branch = matmul(down_kernel, hidden_own, down_weight, width)

    table = tile_table[0].reshape(-1)
    strip_rows = rows_local * enc_size // 2 + 2
    out_rows = rows_local // 2 + 1
    messages = pl.pallas_call(
        functools.partial(project_kernel, enc_size),
        grid_spec=pltpu.PrefetchScalarGridSpec(
            num_scalar_prefetch=2,
            grid=(slots,),
            in_specs=[
                pl.BlockSpec(
                    (1, half, 1, TS, width), lambda s, w, t: (s, 0, w[1], 0, 0)
                ),
                pl.BlockSpec((per_slot, width), lambda s, w, t: (s, 0)),
                pl.BlockSpec((per_slot, width), lambda s, w, t: (s, 0)),
                pl.BlockSpec((1, width), lambda s, w, t: (0, 0)),
                pl.BlockSpec((width, channels), lambda s, w, t: (0, 0)),
            ],
            out_specs=[
                pl.BlockSpec((out_rows * band, channels), lambda s, w, t: (0, 0))
            ]
            * enc_size,
            scratch_shapes=[
                pltpu.VMEM((strip_rows, band, channels), F32),
                pltpu.VMEM((strip_rows, band, 128), F32),
            ],
        ),
        out_shape=[jax.ShapeDtypeStruct((out_rows * band, channels), BF16)] * enc_size,
        compiler_params=PARAMS,
        name="project",
    )(where, table, tok, branch, received, gain_post.reshape(1, -1), w_neck)
    swap = lambda value, step: lax.ppermute(
        value, "enc", [(i, i ^ step) for i in range(enc_size)]
    )
    parts = [messages[0]] + [swap(messages[k], k) for k in range(1, enc_size)]

    sides = 1 if dec_size == 2 else 2
    edge_shape = jax.ShapeDtypeStruct((EDGE, channels), BF16)
    strip, *edges = pl.pallas_call(
        functools.partial(merge_kernel, sides),
        in_specs=[SMEM] + [VMEM] * enc_size,
        out_specs=[VMEM] * (1 + sides),
        out_shape=[jax.ShapeDtypeStruct((out_rows * band, channels), BF16)]
        + [edge_shape] * sides,
        compiler_params=PARAMS,
        name="merge",
    )(where, *[near(value) for value in parts])
    strip_other = flip(strip, "mp")
    flat = lambda dd, mm: dd * 2 + mm
    halo = []
    for side in range(sides):
        for cross in range(2):
            if sides == 1:
                pairs = [
                    (flat(i, c), flat(i ^ 1, c ^ cross)) for i in range(dec_size) for c in range(2)
                ]
            else:
                by = 1 if side == 0 else -1
                pairs = [
                    (flat(i, c), flat(i + by, c ^ cross))
                    for i in range(dec_size)
                    for c in range(2)
                    if 0 <= i + by < dec_size
                ]
            halo.append(lax.ppermute(edges[side], ("dec", "mp"), pairs))
    turns = max(1, rows_local // enc_size)
    logits_parts = pl.pallas_call(
        functools.partial(conv_kernel, enc_size, sides, band),
        in_specs=[SMEM] + [VMEM] * (9 + 2 * sides),
        out_specs=[VMEM] * enc_size,
        out_shape=[jax.ShapeDtypeStruct((turns, classes, band), F32)] * enc_size,
        scratch_shapes=[
            pltpu.VMEM((out_rows, 2, PAD + band + PAD, channels), F32),
            pltpu.VMEM((rows_local, classes, band), F32),
        ],
        compiler_params=PARAMS,
        name="conv",
    )(
        where, near(strip), near(strip_other), near(conv_weight), near(conv_other), bias, bias_other, cls_t,
        cls_other, cls_bias.reshape(-1, 1), *[near(value) for value in halo],
    )
    dealt = [logits_parts[0]] + [swap(logits_parts[k], k) for k in range(1, enc_size)]
    logits, nll = pl.pallas_call(
        functools.partial(loss_kernel, enc_size),
        in_specs=[SMEM] + [VMEM] * (1 + enc_size),
        out_specs=[VMEM] * 2,
        out_shape=[
            jax.ShapeDtypeStruct((rows_local, classes, 1, band), F32),
            jax.ShapeDtypeStruct((rows_local, 1, band), F32),
        ],
        compiler_params=PARAMS,
        name="loss",
    )(where, labels, *[near(value) for value in dealt])
    return (jnp.transpose(logits, (0, 2, 3, 1)), nll)


def solution(mesh):
    in_specs = (
        P(("groups", "dec"), "enc", None, None, None),
        P(),
        P("enc", "mp"),
        P("mp", "enc"),
        P(),
        P(),
        P(None, None, None, "mp"),
        P("mp"),
        P("mp", None),
        P(),
        P(("groups", "dec"), None, None),
        P(None, "enc", ("groups", "dec")),
    )
    out_specs = (P(None, "enc", ("groups", "dec"), None), P(None, "enc", ("groups", "dec")))
    return jax.shard_map(segment, mesh=mesh, in_specs=in_specs, out_specs=out_specs, check_vma=False)
```

```python
import functools

import jax
import jax.numpy as jnp
from jax import lax
from jax.experimental import pallas as pl
from jax.experimental.pallas import tpu as pltpu
from jax.sharding import PartitionSpec as P


TS = 16
PAD = 8

norm_eps = 1e-05
blend_sigma = 4.0

F32 = jnp.float32
BF16 = jnp.bfloat16


VMEM = pl.BlockSpec(memory_space=pltpu.VMEM)
SMEM = pl.BlockSpec(memory_space=pltpu.SMEM)
ANY = pl.BlockSpec(memory_space=pl.ANY)
PARAMS = pltpu.CompilerParams(vmem_limit_bytes=24 * 1024 * 1024)


def near(value):
    return pltpu.with_memory_space_constraint(value, pltpu.VMEM)


def far_memory(value):
    return pltpu.with_memory_space_constraint(value, pltpu.HBM)


def flip(value, axis):
    size = lax.axis_size(axis)
    return lax.ppermute(value, axis, [(i, i ^ 1) for i in range(size)])


def fold_order(size):
    return [0] + list(range(1, size, 2)) + list(range(size - 2 + size % 2, 0, -2))


def ring(value, axis):
    size = lax.axis_size(axis)
    order = fold_order(size)
    return lax.ppermute(
        value, axis, [(order[i], order[(i + 1) % size]) for i in range(size)]
    )


def fold_plane(z, step, size):
    place = jnp.where(z % 2 == 1, (z + 1) // 2, jnp.where(z == 0, 0, size - z // 2))
    place = (place - step + size) % size
    return jnp.where(
        place == 0, 0, jnp.where(place <= size // 2, 2 * place - 1, 2 * (size - place))
    )


def gather_pieces(quarter, far, turn, far_steps):
    size = lax.axis_size("enc")
    pieces = []
    moving = quarter
    for step in range(1, size):
        moving = ring(moving, "enc")
        if far is None:
            pieces.append(moving)
            continue
        across = flip(moving, "dec")
        along = flip(moving, "groups")
        if step <= far_steps:
            far = both = ring(far, "enc")
        elif (step + turn) % 2:
            both = flip(along, "dec")
        else:
            both = flip(across, "groups")
        pieces += [moving, across, along, both]
    return pieces


def spread_of(rows):
    return 4 if rows % 64 == 0 else 1


def cut_kernel(parts, far, where, up, down, up_out, down_out, sems):
    rows = up_out.shape[0]
    start = (where[2] ^ far) * rows if parts > 1 else 0
    rows_at = pl.ds(pl.multiple_of(start, rows), rows)
    copies = [
        pltpu.make_async_copy(source.at[rows_at], out, sems.at[index])
        for index, (source, out) in enumerate(((up, up_out), (down, down_out)))
    ]
    for copy in copies:
        copy.start()
    for copy in copies:
        copy.wait()


def assemble_kernel(enc_size, where, own, *rest):
    pieces, target = rest[:-1], rest[-1]
    z, quarter = where[0], where[2]
    rows = own.shape[0]
    kinds = spread_of(rows)
    part = rows // kinds
    target[pl.ds(pl.multiple_of(z * rows, rows), rows), :] = own[...]
    for step in range(1, enc_size):
        plane = fold_plane(z, step, enc_size)
        for kind in range(kinds):
            start = plane * rows
            if kinds > 1:
                start = start + (quarter ^ kind) * part
            rows_at = pl.ds(pl.multiple_of(start, part), part)
            target[rows_at, :] = pieces[kinds * (step - 1) + kind][...]


def norm_kernel(where, tok_ref, gain_ref, out_ref):
    values = tok_ref[...].reshape(out_ref.shape).astype(F32)
    out_ref[...] = normalize(values, gain_ref[...]).astype(BF16)


def normalize(values, gain):
    mean = jnp.mean(values, axis=-1, keepdims=True)
    centered = values - mean
    var = jnp.mean(centered * centered, axis=-1, keepdims=True)
    return centered * lax.rsqrt(var + norm_eps) * gain


def up_kernel(block, normed, weight, *outs):
    for index, out in enumerate(outs):
        rows = out.shape[0]
        for start in range(0, rows, block):
            source = pl.ds(index * rows + start, block)
            pre = jnp.dot(normed[source, :], weight[...], preferred_element_type=F32)
            out[start : start + block, :] = (
                0.5 * pre * (1.0 + lax.erf(pre * (0.5**0.5)))
            ).astype(BF16)


def down_kernel(block, hidden, weight, *outs):
    for index, out in enumerate(outs):
        rows = out.shape[0]
        for start in range(0, rows, block):
            source = pl.ds(index * rows + start, block)
            out[start : start + block, :] = lax.dot_general(
                hidden[source, :],
                weight[...],
                (((1,), (1,)), ((), ())),
                preferred_element_type=F32,
            ).astype(BF16)


def blend_weight(m, lanes):
    shape = (TS // 2, TS, lanes)
    row = (2 * lax.broadcasted_iota(jnp.int32, shape, 0) + m).astype(F32)
    col = lax.broadcasted_iota(jnp.int32, shape, 1).astype(F32)
    middle = (TS - 1) / 2.0
    spread = ((row - middle) ** 2 + (col - middle) ** 2) / (2.0 * blend_sigma * blend_sigma)
    return jnp.exp(-spread).astype(BF16).astype(F32)


def place_of(table, entry):
    top, left = table[2 * entry], table[2 * entry + 1]
    return top >= 0, pl.ds(top // 2 + 1, TS // 2), pl.ds(pl.multiple_of(left, 8), TS)


def den_kernel(entries, where, table, den):
    weight = blend_weight(where[1], den.shape[2])
    den[...] = jnp.zeros_like(den)
    den[0] = jnp.ones_like(den[0])
    den[den.shape[0] - 1] = jnp.ones_like(den[0])

    def add_entry(entry, carry):
        live, rows, cols = place_of(table, entry)

        @pl.when(live)
        def _():
            den[rows, cols, :] = den[rows, cols, :] + weight

        return carry

    lax.fori_loop(0, entries, add_entry, 0)


def project_kernel(slots, sides, where, table, tok, own, first, second, *rest):
    (gain, neck, den), rest = rest[:3], rest[3:]
    bodies, edges, acc = rest[:2], rest[2:-1], rest[-1]
    z, m = where[0], where[1]
    half = TS // 2
    per_slot = half * TS
    channels = neck.shape[1]
    acc[...] = jnp.zeros_like(acc)
    weight = blend_weight(m, channels)

    def step(slot, carry, other, begin):
        part = pl.ds(pl.multiple_of(slot * per_slot, per_slot), per_slot)
        there = pl.ds(pl.multiple_of((slot - begin) * per_slot, per_slot), per_slot)
        branch = own[part, :].astype(F32) + other[there, :].astype(F32)
        values = tok[slot, :, m].reshape(branch.shape).astype(F32) + branch
        features = normalize(values, gain[...]).astype(BF16)
        maps = jnp.dot(features, neck[...], preferred_element_type=F32).astype(BF16)
        maps = maps.astype(F32).reshape(half, TS, channels)
        live, rows, cols = place_of(table, z * slots + slot)

        @pl.when(live)
        def _():
            acc[rows, cols, :] = acc[rows, cols, :] + maps * weight

        return carry

    middle = slots // 2
    lax.fori_loop(0, middle, functools.partial(step, other=first, begin=0), 0)
    lax.fori_loop(middle, slots, functools.partial(step, other=second, begin=middle), 0)
    quarter = (acc.shape[0] - 2) // 2
    last = acc.shape[1] - 1
    for index, out in enumerate(bodies):
        who = m if index == 0 else 1 - m
        rows = pl.ds(who * quarter + (1 - m), quarter + 1)
        below = den[rows]
        below = jnp.concatenate([below] * (channels // below.shape[2]), axis=2)
        ratio = acc[rows] / below
        out[...] = ratio.reshape(out.shape).astype(BF16)
        left, right = ratio[:, 0, :], ratio[:, last, :]
        if sides == 1:
            columns = (jnp.where(where[3] % 2 == 0, right, left),)
        else:
            columns = (right, left)
        for side, column in enumerate(columns):
            edges[2 * side + index][: quarter + 1] = column.astype(BF16)


def conv_kernel(enc_size, sides, band, where, own, other, conv_own, conv_other, *rest):
    edges, outs, (grid, sums) = rest[: 2 * sides], rest[2 * sides : -2], rest[-2:]
    z, m, d = where[0], where[1], where[3]
    rows = own.shape[0] // band
    channels = own.shape[1]
    half = conv_own.shape[3]
    grid[...] = jnp.zeros_like(grid)
    for who, (strip, lane) in enumerate(((own, 1 - m), (other, m))):
        grid[:, lane, PAD : PAD + band, :] = strip[...].astype(F32).reshape(
            rows, band, channels
        )
        for side in range(sides):
            edge = edges[2 * side + who][...].astype(F32)[:rows].reshape(rows, 1, channels)
            if sides == 2:
                place = PAD - 1 if side == 0 else PAD + band
                grid[:, lane, place : place + 1, :] = edge
            else:

                @pl.when(d % 2 == 1)
                def _():
                    grid[:, lane, PAD - 1 : PAD, :] = edge

                @pl.when(d % 2 == 0)
                def _():
                    grid[:, lane, PAD + band : PAD + band + 1, :] = edge

    count = 2 * rows - 2
    total = jnp.zeros((count * band, 2 * half), F32)
    for col_off in range(3):
        start = PAD - 1 + col_off
        window = grid[:, :, start : start + band, :].reshape(2 * rows, band, channels)
        for row_off in range(3):
            lhs = window[row_off : row_off + count].reshape(count * band, channels)
            both = (conv_own[row_off, col_off], conv_other[row_off, col_off])
            total = total + jnp.dot(
                lhs.astype(BF16), jnp.concatenate(both, axis=1), preferred_element_type=F32
            )
    sums[...] = total.reshape(count, band, 2 * half)
    for step, out in enumerate(outs):
        for turn in range(count // enc_size):
            out[turn * band : (turn + 1) * band, :] = sums[
                (z ^ step) + turn * enc_size
            ].astype(BF16)


def classify_kernel(
    band, where, bias_own, bias_other, cls_own, cls_other, cls_bias, labels, *rest
):
    parts, out = rest[:-1], rest[-1]
    m = where[1]
    total = parts[0][...].astype(F32)
    for part in parts[1:]:
        total = total + part[...].astype(F32)
    half = bias_own.shape[1]
    lines = lax.broadcasted_iota(jnp.int32, (cls_own.shape[0], 1), 0)
    result = jnp.zeros(lines.shape, F32)
    for line in range(cls_own.shape[0]):
        result = jnp.where(lines == line, cls_bias[line], result)
    for which, (bias, cls) in enumerate(((bias_own, cls_own), (bias_other, cls_other))):
        activ = total[:, which * half : (which + 1) * half] + bias[...]
        activ = jnp.maximum(activ, 0.0).astype(BF16)
        result = result + lax.dot_general(
            cls[...], activ, (((1,), (1,)), ((), ())), preferred_element_type=F32
        )
    count = cls_own.shape[0]
    turns = out.shape[0]
    for turn in range(turns):
        logits = result[:, turn * band : (turn + 1) * band]
        label = labels[m * turns + turn]
        classes = lax.broadcasted_iota(jnp.int32, logits.shape, 0)
        picked = jnp.sum(jnp.where(label == classes, logits, 0.0), axis=0, keepdims=True)
        out[turn, :count, :] = logits
        out[turn, count : count + 1, :] = (
            jnp.log(jnp.sum(jnp.exp(logits), axis=0, keepdims=True)) - picked
        )


def deal_kernel(where, own, other, logits_ref, nll_ref):
    m = where[1]
    turns = own.shape[0]
    count = logits_ref.shape[1]
    for who, part in ((m, own), (1 - m, other)):
        for turn in range(turns):
            logits_ref[who * turns + turn, :, 0, :] = part[turn, :count, :]
            nll_ref[who * turns + turn] = part[turn, count : count + 1, :]


def segment(
    tokens,
    gain_pre,
    w_up,
    w_down,
    gain_post,
    w_neck,
    conv_weight,
    conv_bias,
    cls_weight,
    cls_bias,
    tile_table,
    labels,
):
    enc_size = lax.axis_size("enc")
    dec_size = lax.axis_size("dec")
    slots, width = tokens.shape[1], tokens.shape[4]
    ff = w_up.shape[1]
    channels = w_neck.shape[1]
    rows_local, band = labels.shape[0], labels.shape[2]
    classes = cls_weight.shape[1]
    half = TS // 2
    z, m, d = lax.axis_index("enc"), lax.axis_index("mp"), lax.axis_index("dec")
    quarter = (lax.axis_index("groups") % 2) * 2 + d % 2
    where = jnp.stack([z, m, quarter, d]).astype(jnp.int32)

    down_t = w_down.T
    kinds = spread_of(w_up.shape[0])
    part = w_up.shape[0] // kinds

    def cut(far):
        return pl.pallas_call(
            functools.partial(cut_kernel, kinds, far),
            in_specs=[SMEM, ANY, ANY],
            out_specs=[VMEM] * 2,
            out_shape=[jax.ShapeDtypeStruct((part, ff), BF16)] * 2,
            scratch_shapes=[pltpu.SemaphoreType.DMA((2,))],
            compiler_params=PARAMS,
        )(where, far_memory(w_up), far_memory(down_t))

    first = cut(0)
    far = cut(3) if kinds > 1 else (None, None)
    up_pieces = gather_pieces(first[0], far[0], 1, 1)
    down_pieces = gather_pieces(first[1], far[1], 1, 1)
    conv_other = flip(conv_weight, "mp")
    cls_t = cls_weight.T
    cls_other = flip(cls_t, "mp")
    bias = conv_bias.reshape(1, -1)
    bias_other = flip(bias, "mp")

    tok = tokens.reshape(slots, half, 2, TS, width)
    per_slot = half * TS
    count = slots * per_slot
    halves = {"own": lambda w: w[1], "other": lambda w: 1 - w[1]}

    def norm(which):
        return pl.pallas_call(
            norm_kernel,
            grid_spec=pltpu.PrefetchScalarGridSpec(
                num_scalar_prefetch=1,
                grid=(slots // 2,),
                in_specs=[
                    pl.BlockSpec(
                        (2, half, 1, TS, width),
                        lambda s, w: (s, 0, halves[which](w), 0, 0),
                    ),
                    pl.BlockSpec((1, width), lambda s, w: (0, 0)),
                ],
                out_specs=pl.BlockSpec((2 * per_slot, width), lambda s, w: (s, 0)),
            ),
            out_shape=pltpu.VMEM((count, width), BF16),
            compiler_params=PARAMS,
        )(where, tok, gain_pre.reshape(1, -1))

    def assembled(shard, pieces):
        return pl.pallas_call(
            functools.partial(assemble_kernel, enc_size),
            in_specs=[SMEM] + [VMEM] * (1 + len(pieces)),
            out_specs=VMEM,
            out_shape=jax.ShapeDtypeStruct((shard.shape[0] * enc_size, ff), BF16),
            compiler_params=PARAMS,
        )(where, near(shard), *[near(value) for value in pieces])

    block = 512

    def matmul(kernel, value, weight, columns, outs=1):
        rows = value.shape[0] // outs
        return pl.pallas_call(
            functools.partial(kernel, min(block, rows)),
            in_specs=[VMEM] * 2,
            out_specs=[VMEM] * outs,
            out_shape=[jax.ShapeDtypeStruct((rows, columns), BF16)] * outs,
            compiler_params=PARAMS,
        )(near(value), near(weight))

    normed_other = norm("other")
    normed_own = norm("own")
    up_weight = assembled(w_up, up_pieces)
    hidden_other = matmul(up_kernel, normed_other, up_weight, ff, 2)
    hidden_own = matmul(up_kernel, normed_own, up_weight, ff)
    down_weight = assembled(down_t, down_pieces)
    received = []
    for hidden in hidden_other:
        part_other = matmul(down_kernel, hidden, down_weight, width)[0]
        received.append(flip(part_other, "mp"))
    branch = matmul(down_kernel, hidden_own[0], down_weight, width)[0]

    table = tile_table[0].reshape(-1)
    strip_rows = rows_local * enc_size // 2 + 2
    den = pl.pallas_call(
        functools.partial(den_kernel, tile_table.shape[1]),
        in_specs=[SMEM] * 2,
        out_specs=VMEM,
        out_shape=jax.ShapeDtypeStruct((strip_rows, band, 128), F32),
        compiler_params=PARAMS,
        name="den",
    )(where, table)
    sides = 1 if dec_size == 2 else 2
    piece_rows = strip_rows // 2
    strip_shape = jax.ShapeDtypeStruct((piece_rows * band, channels), BF16)
    edge_shape = jax.ShapeDtypeStruct(((piece_rows + 15) // 16 * 16, channels), BF16)
    keep, give, *edges = pl.pallas_call(
        functools.partial(project_kernel, slots, sides),
        in_specs=[SMEM] * 2 + [VMEM] * 7,
        out_specs=[VMEM] * (2 + 2 * sides),
        out_shape=[strip_shape] * 2 + [edge_shape] * (2 * sides),
        scratch_shapes=[pltpu.VMEM((strip_rows, band, channels), F32)],
        compiler_params=PARAMS,
        name="project",
    )(
        where, table, near(tok), near(branch), near(received[0]), near(received[1]),
        near(gain_post.reshape(1, -1)), near(w_neck), near(den),
    )
    strip_other = flip(give, "mp")
    flat = lambda dd, mm: dd * 2 + mm
    halo = []
    for side in range(sides):
        for cross in range(2):
            by = 1 if side == 0 else -1
            hop = (lambda i: i ^ 1) if sides == 1 else (lambda i: i + by)
            pairs = [
                (flat(i, c), flat(hop(i), c ^ cross))
                for i in range(dec_size)
                for c in range(2)
                if 0 <= hop(i) < dec_size
            ]
            halo.append(lax.ppermute(edges[2 * side + cross], ("dec", "mp"), pairs))
    turns = rows_local // 2
    messages = pl.pallas_call(
        functools.partial(conv_kernel, enc_size, sides, band),
        in_specs=[SMEM] + [VMEM] * (4 + 2 * sides),
        out_specs=[VMEM] * enc_size,
        out_shape=[jax.ShapeDtypeStruct((turns * band, channels), BF16)] * enc_size,
        scratch_shapes=[
            pltpu.VMEM((piece_rows, 2, PAD + band + PAD, channels), F32),
            pltpu.VMEM((2 * piece_rows - 2, band, channels), F32),
        ],
        compiler_params=PARAMS,
        name="conv",
    )(
        where, near(keep), near(strip_other), near(conv_weight), near(conv_other),
        *[near(value) for value in halo],
    )
    parts = [messages[0]]
    for step in range(1, enc_size):
        parts.append(
            lax.ppermute(
                messages[step], "enc", [(i, i ^ step) for i in range(enc_size)]
            )
        )
    result = pl.pallas_call(
        functools.partial(classify_kernel, band),
        in_specs=[SMEM] + [VMEM] * 4 + [SMEM] + [VMEM] * (1 + enc_size),
        out_specs=VMEM,
        out_shape=jax.ShapeDtypeStruct((turns, classes + 1, band), F32),
        compiler_params=PARAMS,
        name="classify",
    )(
        where, bias, bias_other, cls_t, cls_other, cls_bias, labels,
        *[near(value) for value in parts],
    )
    result_other = flip(result, "mp")
    logits, nll = pl.pallas_call(
        deal_kernel,
        in_specs=[SMEM] + [VMEM] * 2,
        out_specs=[VMEM] * 2,
        out_shape=[
            jax.ShapeDtypeStruct((rows_local, classes, 1, band), F32),
            jax.ShapeDtypeStruct((rows_local, 1, band), F32),
        ],
        compiler_params=PARAMS,
        name="result",
    )(where, near(result), near(result_other))
    return (jnp.transpose(logits, (0, 2, 3, 1)), nll)


def solution(mesh):
    in_specs = (
        P(("groups", "dec"), "enc", None, None, None),
        P(),
        P("enc", "mp"),
        P("mp", "enc"),
        P(),
        P(),
        P(None, None, None, "mp"),
        P("mp"),
        P("mp", None),
        P(),
        P(("groups", "dec"), None, None),
        P(None, "enc", ("groups", "dec")),
    )
    out_specs = (P(None, "enc", ("groups", "dec"), None), P(None, "enc", ("groups", "dec")))
    return jax.shard_map(segment, mesh=mesh, in_specs=in_specs, out_specs=out_specs, check_vma=False)
```

```python
import functools

import jax
import jax.numpy as jnp
from jax import lax
from jax.experimental import pallas as pl
from jax.experimental.pallas import tpu as pltpu
from jax.sharding import PartitionSpec as P


TS = 16
PAD = 8

norm_eps = 1e-05
blend_sigma = 4.0

F32 = jnp.float32
BF16 = jnp.bfloat16


VMEM = pl.BlockSpec(memory_space=pltpu.VMEM)
SMEM = pl.BlockSpec(memory_space=pltpu.SMEM)
ANY = pl.BlockSpec(memory_space=pl.ANY)
PARAMS = pltpu.CompilerParams(vmem_limit_bytes=24 * 1024 * 1024)


def near(value):
    return pltpu.with_memory_space_constraint(value, pltpu.VMEM)


def far_memory(value):
    return pltpu.with_memory_space_constraint(value, pltpu.HBM)


def flip(value, axis):
    size = lax.axis_size(axis)
    return lax.ppermute(value, axis, [(i, i ^ 1) for i in range(size)])


def fold_order(size):
    return [0] + list(range(1, size, 2)) + list(range(size - 2 + size % 2, 0, -2))


def ring(value, axis, by=1):
    size = lax.axis_size(axis)
    order = fold_order(size)
    return lax.ppermute(
        value, axis, [(order[i], order[(i + by) % size]) for i in range(size)]
    )


def fold_plane(z, step, size):
    place = jnp.where(z % 2 == 1, (z + 1) // 2, jnp.where(z == 0, 0, size - z // 2))
    place = (place - step + size) % size
    return jnp.where(
        place == 0, 0, jnp.where(place <= size // 2, 2 * place - 1, 2 * (size - place))
    )


def gather_pieces(quarter, far, turn):
    size = lax.axis_size("enc")
    pieces = []
    moving = quarter
    for step in range(1, size):
        moving = ring(moving, "enc")
        if far is None:
            pieces.append(moving)
            continue
        across = flip(moving, "dec")
        along = flip(moving, "groups")
        if step == size - 1:
            both = ring(far, "enc", -1)
        elif (step + turn) % 2:
            both = flip(along, "dec")
        else:
            both = flip(across, "groups")
        pieces += [moving, across, along, both]
    return pieces


def spread_of(rows):
    return 4 if rows % 64 == 0 else 1


def cut_kernel(parts, far, where, up, down, up_out, down_out, sems):
    rows = up_out.shape[0]
    start = (where[2] ^ far) * rows if parts > 1 else 0
    rows_at = pl.ds(pl.multiple_of(start, rows), rows)
    copies = [
        pltpu.make_async_copy(source.at[rows_at], out, sems.at[index])
        for index, (source, out) in enumerate(((up, up_out), (down, down_out)))
    ]
    for copy in copies:
        copy.start()
    for copy in copies:
        copy.wait()


def assemble_kernel(enc_size, where, own, *rest):
    pieces, target = rest[:-1], rest[-1]
    z, quarter = where[0], where[2]
    rows = own.shape[0]
    kinds = spread_of(rows)
    part = rows // kinds
    target[pl.ds(pl.multiple_of(z * rows, rows), rows), :] = own[...]
    for step in range(1, enc_size):
        plane = fold_plane(z, step, enc_size)
        for kind in range(kinds):
            start = plane * rows
            if kinds > 1:
                start = start + (quarter ^ kind) * part
            rows_at = pl.ds(pl.multiple_of(start, part), part)
            target[rows_at, :] = pieces[kinds * (step - 1) + kind][...]


def norm_kernel(where, tok_ref, gain_ref, out_ref):
    values = tok_ref[...].reshape(out_ref.shape).astype(F32)
    out_ref[...] = normalize(values, gain_ref[...]).astype(BF16)


def normalize(values, gain):
    mean = jnp.mean(values, axis=-1, keepdims=True)
    centered = values - mean
    var = jnp.mean(centered * centered, axis=-1, keepdims=True)
    return centered * lax.rsqrt(var + norm_eps) * gain


def up_kernel(block, normed, weight, *outs):
    for index, out in enumerate(outs):
        rows = out.shape[0]
        for start in range(0, rows, block):
            source = pl.ds(index * rows + start, block)
            pre = jnp.dot(normed[source, :], weight[...], preferred_element_type=F32)
            out[start : start + block, :] = (
                0.5 * pre * (1.0 + lax.erf(pre * (0.5**0.5)))
            ).astype(BF16)


def down_kernel(block, hidden, weight, *outs):
    for index, out in enumerate(outs):
        rows = out.shape[0]
        for start in range(0, rows, block):
            source = pl.ds(index * rows + start, block)
            out[start : start + block, :] = lax.dot_general(
                hidden[source, :],
                weight[...],
                (((1,), (1,)), ((), ())),
                preferred_element_type=F32,
            ).astype(BF16)


def blend_weight(m, lanes):
    shape = (TS // 2, TS, lanes)
    row = (2 * lax.broadcasted_iota(jnp.int32, shape, 0) + m).astype(F32)
    col = lax.broadcasted_iota(jnp.int32, shape, 1).astype(F32)
    middle = (TS - 1) / 2.0
    spread = ((row - middle) ** 2 + (col - middle) ** 2) / (2.0 * blend_sigma * blend_sigma)
    return jnp.exp(-spread).astype(BF16).astype(F32)


def place_of(table, entry):
    top, left = table[2 * entry], table[2 * entry + 1]
    return top >= 0, pl.ds(top // 2 + 1, TS // 2), pl.ds(pl.multiple_of(left, 8), TS)


def den_kernel(entries, where, table, den):
    weight = blend_weight(where[1], den.shape[2])
    den[...] = jnp.zeros_like(den)
    den[0] = jnp.ones_like(den[0])
    den[den.shape[0] - 1] = jnp.ones_like(den[0])

    def add_entry(entry, carry):
        live, rows, cols = place_of(table, entry)

        @pl.when(live)
        def _():
            den[rows, cols, :] = den[rows, cols, :] + weight

        return carry

    lax.fori_loop(0, entries, add_entry, 0)


def project_kernel(slots, sides, where, table, tok, own, first, second, *rest):
    (gain, neck, den), rest = rest[:3], rest[3:]
    bodies, edges, acc = rest[:2], rest[2:-1], rest[-1]
    z, m = where[0], where[1]
    half = TS // 2
    per_slot = half * TS
    channels = neck.shape[1]
    acc[...] = jnp.zeros_like(acc)
    weight = blend_weight(m, channels)

    def step(slot, carry, other, begin):
        part = pl.ds(pl.multiple_of(slot * per_slot, per_slot), per_slot)
        there = pl.ds(pl.multiple_of((slot - begin) * per_slot, per_slot), per_slot)
        branch = own[part, :].astype(F32) + other[there, :].astype(F32)
        values = tok[slot, :, m].reshape(branch.shape).astype(F32) + branch
        features = normalize(values, gain[...]).astype(BF16)
        maps = jnp.dot(features, neck[...], preferred_element_type=F32).astype(BF16)
        maps = maps.astype(F32).reshape(half, TS, channels)
        live, rows, cols = place_of(table, z * slots + slot)

        @pl.when(live)
        def _():
            acc[rows, cols, :] = acc[rows, cols, :] + maps * weight

        return carry

    middle = slots // 2
    lax.fori_loop(0, middle, functools.partial(step, other=first, begin=0), 0)
    lax.fori_loop(middle, slots, functools.partial(step, other=second, begin=middle), 0)
    quarter = (acc.shape[0] - 2) // 2
    last = acc.shape[1] - 1
    for index, out in enumerate(bodies):
        who = m if index == 0 else 1 - m
        rows = pl.ds(who * quarter + (1 - m), quarter + 1)
        below = den[rows]
        below = jnp.concatenate([below] * (channels // below.shape[2]), axis=2)
        ratio = acc[rows] / below
        out[...] = ratio.reshape(out.shape).astype(BF16)
        left, right = ratio[:, 0, :], ratio[:, last, :]
        if sides == 1:
            columns = (jnp.where(where[3] % 2 == 0, right, left),)
        else:
            columns = (right, left)
        for side, column in enumerate(columns):
            edges[2 * side + index][: quarter + 1] = column.astype(BF16)


def conv_kernel(enc_size, sides, band, where, own, other, conv_own, conv_other, *rest):
    edges, outs, (grid, sums) = rest[: 2 * sides], rest[2 * sides : -2], rest[-2:]
    z, m, d = where[0], where[1], where[3]
    rows = own.shape[0] // band
    channels = own.shape[1]
    half = conv_own.shape[3]
    grid[...] = jnp.zeros_like(grid)
    for who, (strip, lane) in enumerate(((own, 1 - m), (other, m))):
        grid[:, lane, PAD : PAD + band, :] = strip[...].astype(F32).reshape(
            rows, band, channels
        )
        for side in range(sides):
            edge = edges[2 * side + who][...].astype(F32)[:rows].reshape(rows, 1, channels)
            if sides == 2:
                place = PAD - 1 if side == 0 else PAD + band
                grid[:, lane, place : place + 1, :] = edge
            else:

                @pl.when(d % 2 == 1)
                def _():
                    grid[:, lane, PAD - 1 : PAD, :] = edge

                @pl.when(d % 2 == 0)
                def _():
                    grid[:, lane, PAD + band : PAD + band + 1, :] = edge

    count = 2 * rows - 2
    total = jnp.zeros((count * band, 2 * half), F32)
    for col_off in range(3):
        start = PAD - 1 + col_off
        window = grid[:, :, start : start + band, :].reshape(2 * rows, band, channels)
        for row_off in range(3):
            lhs = window[row_off : row_off + count].reshape(count * band, channels)
            both = (conv_own[row_off, col_off], conv_other[row_off, col_off])
            total = total + jnp.dot(
                lhs.astype(BF16), jnp.concatenate(both, axis=1), preferred_element_type=F32
            )
    sums[...] = total.reshape(count, band, 2 * half)
    for step, out in enumerate(outs):
        for turn in range(count // enc_size):
            out[turn * band : (turn + 1) * band, :] = sums[
                (z ^ step) + turn * enc_size
            ].astype(BF16)


def classify_kernel(
    band, where, bias_own, bias_other, cls_own, cls_other, cls_bias, labels, *rest
):
    parts, out = rest[:-1], rest[-1]
    m = where[1]
    total = parts[0][...].astype(F32)
    for part in parts[1:]:
        total = total + part[...].astype(F32)
    half = bias_own.shape[1]
    lines = lax.broadcasted_iota(jnp.int32, (cls_own.shape[0], 1), 0)
    result = jnp.zeros(lines.shape, F32)
    for line in range(cls_own.shape[0]):
        result = jnp.where(lines == line, cls_bias[line], result)
    for which, (bias, cls) in enumerate(((bias_own, cls_own), (bias_other, cls_other))):
        activ = total[:, which * half : (which + 1) * half] + bias[...]
        activ = jnp.maximum(activ, 0.0).astype(BF16)
        result = result + lax.dot_general(
            cls[...], activ, (((1,), (1,)), ((), ())), preferred_element_type=F32
        )
    count = cls_own.shape[0]
    turns = out.shape[0]
    for turn in range(turns):
        logits = result[:, turn * band : (turn + 1) * band]
        label = labels[m * turns + turn]
        classes = lax.broadcasted_iota(jnp.int32, logits.shape, 0)
        picked = jnp.sum(jnp.where(label == classes, logits, 0.0), axis=0, keepdims=True)
        out[turn, :count, :] = logits
        out[turn, count : count + 1, :] = (
            jnp.log(jnp.sum(jnp.exp(logits), axis=0, keepdims=True)) - picked
        )


def deal_kernel(where, own, other, logits_ref, nll_ref):
    m = where[1]
    turns = own.shape[0]
    count = logits_ref.shape[1]
    for who, part in ((m, own), (1 - m, other)):
        for turn in range(turns):
            logits_ref[who * turns + turn, :, 0, :] = part[turn, :count, :]
            nll_ref[who * turns + turn] = part[turn, count : count + 1, :]


def segment(
    tokens,
    gain_pre,
    w_up,
    w_down,
    gain_post,
    w_neck,
    conv_weight,
    conv_bias,
    cls_weight,
    cls_bias,
    tile_table,
    labels,
):
    enc_size = lax.axis_size("enc")
    dec_size = lax.axis_size("dec")
    slots, width = tokens.shape[1], tokens.shape[4]
    ff = w_up.shape[1]
    channels = w_neck.shape[1]
    rows_local, band = labels.shape[0], labels.shape[2]
    classes = cls_weight.shape[1]
    half = TS // 2
    z, m, d = lax.axis_index("enc"), lax.axis_index("mp"), lax.axis_index("dec")
    quarter = (lax.axis_index("groups") % 2) * 2 + d % 2
    where = jnp.stack([z, m, quarter, d]).astype(jnp.int32)

    down_t = w_down.T
    kinds = spread_of(w_up.shape[0])
    part = w_up.shape[0] // kinds

    def cut(far):
        return pl.pallas_call(
            functools.partial(cut_kernel, kinds, far),
            in_specs=[SMEM, ANY, ANY],
            out_specs=[VMEM] * 2,
            out_shape=[jax.ShapeDtypeStruct((part, ff), BF16)] * 2,
            scratch_shapes=[pltpu.SemaphoreType.DMA((2,))],
            compiler_params=PARAMS,
        )(where, far_memory(w_up), far_memory(down_t))

    first = cut(0)
    far = cut(3) if kinds > 1 else (None, None)
    up_pieces = gather_pieces(first[0], far[0], 0)
    down_pieces = gather_pieces(first[1], far[1], 1)
    conv_other = flip(conv_weight, "mp")
    cls_t = cls_weight.T
    cls_other = flip(cls_t, "mp")
    bias = conv_bias.reshape(1, -1)
    bias_other = flip(bias, "mp")

    tok = tokens.reshape(slots, half, 2, TS, width)
    per_slot = half * TS
    count = slots * per_slot
    halves = {"own": lambda w: w[1], "other": lambda w: 1 - w[1]}

    def norm(which):
        return pl.pallas_call(
            norm_kernel,
            grid_spec=pltpu.PrefetchScalarGridSpec(
                num_scalar_prefetch=1,
                grid=(slots // 2,),
                in_specs=[
                    pl.BlockSpec(
                        (2, half, 1, TS, width),
                        lambda s, w: (s, 0, halves[which](w), 0, 0),
                    ),
                    pl.BlockSpec((1, width), lambda s, w: (0, 0)),
                ],
                out_specs=pl.BlockSpec((2 * per_slot, width), lambda s, w: (s, 0)),
            ),
            out_shape=pltpu.VMEM((count, width), BF16),
            compiler_params=PARAMS,
        )(where, tok, gain_pre.reshape(1, -1))

    def assembled(shard, pieces):
        return pl.pallas_call(
            functools.partial(assemble_kernel, enc_size),
            in_specs=[SMEM] + [VMEM] * (1 + len(pieces)),
            out_specs=VMEM,
            out_shape=jax.ShapeDtypeStruct((shard.shape[0] * enc_size, ff), BF16),
            compiler_params=PARAMS,
        )(where, near(shard), *[near(value) for value in pieces])

    block = 512

    def matmul(kernel, value, weight, columns, outs=1):
        rows = value.shape[0] // outs
        return pl.pallas_call(
            functools.partial(kernel, min(block, rows)),
            in_specs=[VMEM] * 2,
            out_specs=[VMEM] * outs,
            out_shape=[jax.ShapeDtypeStruct((rows, columns), BF16)] * outs,
            compiler_params=PARAMS,
        )(near(value), near(weight))

    normed_other = norm("other")
    normed_own = norm("own")
    up_weight = assembled(w_up, up_pieces)
    hidden_other = matmul(up_kernel, normed_other, up_weight, ff, 2)
    hidden_own = matmul(up_kernel, normed_own, up_weight, ff)
    down_weight = assembled(down_t, down_pieces)
    received = []
    for hidden in hidden_other:
        part_other = matmul(down_kernel, hidden, down_weight, width)[0]
        received.append(flip(part_other, "mp"))
    branch = matmul(down_kernel, hidden_own[0], down_weight, width)[0]

    table = tile_table[0].reshape(-1)
    strip_rows = rows_local * enc_size // 2 + 2
    den = pl.pallas_call(
        functools.partial(den_kernel, tile_table.shape[1]),
        in_specs=[SMEM] * 2,
        out_specs=VMEM,
        out_shape=jax.ShapeDtypeStruct((strip_rows, band, 128), F32),
        compiler_params=PARAMS,
        name="den",
    )(where, table)
    sides = 1 if dec_size == 2 else 2
    piece_rows = strip_rows // 2
    strip_shape = jax.ShapeDtypeStruct((piece_rows * band, channels), BF16)
    edge_shape = jax.ShapeDtypeStruct(((piece_rows + 15) // 16 * 16, channels), BF16)
    keep, give, *edges = pl.pallas_call(
        functools.partial(project_kernel, slots, sides),
        in_specs=[SMEM] * 2 + [VMEM] * 7,
        out_specs=[VMEM] * (2 + 2 * sides),
        out_shape=[strip_shape] * 2 + [edge_shape] * (2 * sides),
        scratch_shapes=[pltpu.VMEM((strip_rows, band, channels), F32)],
        compiler_params=PARAMS,
        name="project",
    )(
        where, table, near(tok), near(branch), near(received[0]), near(received[1]),
        near(gain_post.reshape(1, -1)), near(w_neck), near(den),
    )
    strip_other = flip(give, "mp")
    flat = lambda dd, mm: dd * 2 + mm
    halo = []
    for side in range(sides):
        for cross in range(2):
            by = 1 if side == 0 else -1
            hop = (lambda i: i ^ 1) if sides == 1 else (lambda i: i + by)
            pairs = [
                (flat(i, c), flat(hop(i), c ^ cross))
                for i in range(dec_size)
                for c in range(2)
                if 0 <= hop(i) < dec_size
            ]
            halo.append(lax.ppermute(edges[2 * side + cross], ("dec", "mp"), pairs))
    turns = rows_local // 2
    messages = pl.pallas_call(
        functools.partial(conv_kernel, enc_size, sides, band),
        in_specs=[SMEM] + [VMEM] * (4 + 2 * sides),
        out_specs=[VMEM] * enc_size,
        out_shape=[jax.ShapeDtypeStruct((turns * band, channels), BF16)] * enc_size,
        scratch_shapes=[
            pltpu.VMEM((piece_rows, 2, PAD + band + PAD, channels), F32),
            pltpu.VMEM((2 * piece_rows - 2, band, channels), F32),
        ],
        compiler_params=PARAMS,
        name="conv",
    )(
        where, near(keep), near(strip_other), near(conv_weight), near(conv_other),
        *[near(value) for value in halo],
    )
    parts = [messages[0]]
    for step in range(1, enc_size):
        parts.append(
            lax.ppermute(
                messages[step], "enc", [(i, i ^ step) for i in range(enc_size)]
            )
        )
    result = pl.pallas_call(
        functools.partial(classify_kernel, band),
        in_specs=[SMEM] + [VMEM] * 4 + [SMEM] + [VMEM] * (1 + enc_size),
        out_specs=VMEM,
        out_shape=jax.ShapeDtypeStruct((turns, classes + 1, band), F32),
        compiler_params=PARAMS,
        name="classify",
    )(
        where, bias, bias_other, cls_t, cls_other, cls_bias, labels,
        *[near(value) for value in parts],
    )
    result_other = flip(result, "mp")
    logits, nll = pl.pallas_call(
        deal_kernel,
        in_specs=[SMEM] + [VMEM] * 2,
        out_specs=[VMEM] * 2,
        out_shape=[
            jax.ShapeDtypeStruct((rows_local, classes, 1, band), F32),
            jax.ShapeDtypeStruct((rows_local, 1, band), F32),
        ],
        compiler_params=PARAMS,
        name="result",
    )(where, near(result), near(result_other))
    return (jnp.transpose(logits, (0, 2, 3, 1)), nll)


def solution(mesh):
    in_specs = (
        P(("groups", "dec"), "enc", None, None, None),
        P(),
        P("enc", "mp"),
        P("mp", "enc"),
        P(),
        P(),
        P(None, None, None, "mp"),
        P("mp"),
        P("mp", None),
        P(),
        P(("groups", "dec"), None, None),
        P(None, "enc", ("groups", "dec")),
    )
    out_specs = (P(None, "enc", ("groups", "dec"), None), P(None, "enc", ("groups", "dec")))
    return jax.shard_map(segment, mesh=mesh, in_specs=in_specs, out_specs=out_specs, check_vma=False)
```
